128 devices in a mesh: rows: 8 (over z, x_hi), protos: 16 (over y, x_lo, core).
Axes of the slice: x: 4 (x_hi: 2, x_lo: 2; x = x_hi * 2 + x_lo), y: 4, z: 4, core: 2. Of those that a mesh axis runs over, the one named last changes fastest.
Arguments:
- teacher_rows: bfloat16 [8192, 256], P(('rows', 'protos')), may hold values from -16 to 16
- student_rows: bfloat16 [8192, 256], P(('rows', 'protos')), may hold values from -16 to 16
- prototypes: bfloat16 [256, 131072], P(None, 'protos'), may hold values from -16 to 16
Outputs:
- row_grads: float32 [8192, 256], P(('rows', 'protos'))
- row_loss: float32 [8192], P(('rows', 'protos'))
The draws below stay inside these ranges and needn't reach their ends.
All inputs are finite; a program needn't handle non-finite values.
Results may differ from the reference program's by a relative error of at most 0.0015.
Values may be sent and summed in bfloat16 or wider, within the bound.
A program may use at most 192 MiB of HBM per device.

```python
import jax
import jax.numpy as jnp
from jax import lax

BOTTLE = 256
PROTOTYPES = 131072
ITERS = 3
BATCH = 8192


def center_table(key):
    return jax.random.truncated_normal(jax.random.fold_in(key, 101), -4.0, 4.0, (16, BOTTLE), jnp.float32)


def crop_labels(key):
    cuts = jax.random.randint(jax.random.fold_in(key, 102), (15,), 0, BATCH)
    positions = jnp.arange(BATCH, dtype=jnp.int32)
    segment = jnp.sum((positions[:, None] >= cuts[None, :]).astype(jnp.int32), axis=1)
    order = jax.random.permutation(jax.random.fold_in(key, 110), 16)
    return order[segment]


def crop_mixture(key):
    centers = center_table(key)
    labels = crop_labels(key)
    following = (labels + 1) % 16
    return centers[labels] + centers[following]


def draw_teacher_rows(key, part):
    mixture = crop_mixture(key)
    noise = jax.random.truncated_normal(jax.random.fold_in(key, 103), -4.0, 4.0, (BATCH, BOTTLE), jnp.float32)
    strength = jnp.full((BATCH, 1), 0.85, jnp.float32)
    return (noise + strength * mixture).astype(jnp.bfloat16)


def draw_student_rows(key, part):
    mixture = crop_mixture(key)
    noise = jax.random.truncated_normal(jax.random.fold_in(key, 105), -4.0, 4.0, (BATCH, BOTTLE), jnp.float32)
    strength = jnp.full((BATCH, 1), 0.7, jnp.float32)
    return (noise + strength * mixture).astype(jnp.bfloat16)


def draw_prototypes(key, part):
    centers = center_table(key)
    labels = jax.random.randint(jax.random.fold_in(key, 107), (PROTOTYPES,), 0, 16)
    noise = jax.random.truncated_normal(jax.random.fold_in(key, 108), -4.0, 4.0, (BOTTLE, PROTOTYPES), jnp.float32)
    position = jnp.arange(PROTOTYPES, dtype=jnp.float32)[None, :] / (PROTOTYPES - 1.0)
    strength = 0.2 + 0.8 * position
    return (noise + strength * jnp.transpose(centers[labels])).astype(jnp.bfloat16)


def setup_inputs(seed: int = 0) -> dict:
    streams_of = jax.random.split(jax.random.key(seed), 4)
    teacher_rows = draw_teacher_rows(jax.random.fold_in(streams_of[3], 71), 0)
    student_rows = draw_student_rows(jax.random.fold_in(streams_of[3], 71), 0)
    prototypes = draw_prototypes(jax.random.fold_in(streams_of[3], 71), 0)
    return dict(teacher_rows=teacher_rows, student_rows=student_rows, prototypes=prototypes)


EPSILON = 1e-06
TEACHER_TEMP = 0.04
STUDENT_TEMP = 0.1

def unit_rows(values):
    floats = values.astype(jnp.float32)
    norms = jnp.sqrt(lax.optimization_barrier(jnp.sum(floats * floats, axis=1, keepdims=True)) + EPSILON)
    return (floats / norms, norms)

def reference(teacher_rows, student_rows, prototypes):
    proto_float = prototypes.astype(jnp.float32)
    proto_norm = jnp.sqrt(lax.optimization_barrier(jnp.sum(proto_float * proto_float, axis=0, keepdims=True)) + EPSILON)
    proto_unit = proto_float / proto_norm
    proto_half = proto_unit.astype(jnp.bfloat16)
    teacher_unit = unit_rows(teacher_rows)[0]
    student_float, student_norm = unit_rows(student_rows)
    student_unit = student_float.astype(jnp.bfloat16)
    nblocks = 16
    width = PROTOTYPES // nblocks
    blocks_full = jnp.transpose(proto_unit.reshape(BOTTLE, nblocks, width), (1, 0, 2))
    blocks_half = jnp.transpose(proto_half.reshape(BOTTLE, nblocks, width), (1, 0, 2))

    def teacher_block(block):
        return jnp.exp(jnp.dot(teacher_unit, block, precision=lax.Precision.HIGHEST, preferred_element_type=jnp.float32) / TEACHER_TEMP)

    def student_block(block):
        return jnp.dot(student_unit, block, preferred_element_type=jnp.float32) / STUDENT_TEMP
    weights = jnp.ones((BATCH,), jnp.float32)
    inverse = jnp.ones((PROTOTYPES,), jnp.float32)
    for sweep in range(ITERS):
        columns = lax.map(lambda block: lax.optimization_barrier(jnp.sum(teacher_block(block) * weights[:, None], axis=0)), blocks_full)
        inverse = 1.0 / columns.reshape(PROTOTYPES)
        inverse_blocks = inverse.reshape(nblocks, width)
        partial_rows = lax.map(lambda pair: lax.optimization_barrier(jnp.sum(teacher_block(pair[0]) * pair[1][None, :], axis=1)), (blocks_full, inverse_blocks))
        weights = 1.0 / lax.optimization_barrier(jnp.sum(partial_rows, axis=0))
    totals = lax.map(lambda block: lax.optimization_barrier(jnp.sum(jnp.exp(student_block(block)), axis=1)), blocks_half)
    sample_total = lax.optimization_barrier(jnp.sum(totals, axis=0))
    inverse_blocks = inverse.reshape(nblocks, width)

    def accumulate(carry, triple):
        grad_acc, loss_acc = carry
        block_full, block_half, inv_block = triple
        targets = teacher_block(block_full) * inv_block[None, :] * weights[:, None]
        logits = student_block(block_half)
        signal = (jnp.exp(logits) / sample_total[:, None] - targets).astype(jnp.bfloat16)
        grad_acc = grad_acc + lax.dot_general(signal, block_half, (((1,), (1,)), ((), ())), preferred_element_type=jnp.float32)
        loss_acc = loss_acc + lax.optimization_barrier(jnp.sum(targets * logits, axis=1))
        return ((grad_acc, loss_acc), None)
    start = (jnp.zeros((BATCH, BOTTLE), jnp.float32), jnp.zeros((BATCH,), jnp.float32))
    (grad_sum, cross), unused = lax.scan(accumulate, start, (blocks_full, blocks_half, inverse_blocks))
    direction = grad_sum / STUDENT_TEMP
    radial = lax.optimization_barrier(jnp.sum(student_float * direction, axis=1, keepdims=True))
    row_grads = (direction - student_float * radial) / student_norm
    row_loss = jnp.log(sample_total) - cross
    return (row_grads, row_loss)
```

```python
import functools
import math

import jax
import jax.numpy as jnp
from jax import lax
from jax.experimental import pallas as pl
from jax.experimental.pallas import tpu as pltpu
from jax.sharding import PartitionSpec as P

ITERS = 3
EPSILON = 1e-06
TEACHER_TEMP = 0.04
STUDENT_TEMP = 0.1
LOG2E = math.log2(math.e)

R = 8
NP = 16
Y = 4
OWN = 64
PLANE = 256
ROWS = 1024
D = 256
K = 8192
LANES = 128
NCH = 4
CW = K // NCH
CT = CW // LANES
KT = K // LANES
KE = 1024
MESH = pl.DeviceIdType.MESH
NT = (((1,), (1,)), ((), ()))


def kernel(
    tea_hbm, stu_hbm, pro_hbm,
    grad_ref, loss_ref,
    exps, proto, half, tea, stu, unit,
    tscale, wexp, racc, sacc, own_buf,
    rnorm, invb, colp, colr, rowr,
    ga, gb, pxa, pxb, psa, psb, rsa, rsb, tota, totb,
    load_sem, g_send, g_recv, c_send, c_recv, r_send, r_recv,
    t_send, t_recv, p_send, p_recv, s_send, s_recv,
):
    r = lax.axis_index("rows")
    p = lax.axis_index("protos")
    y, x, c = p // 4, (p // 2) % 2, p % 2
    pc = 1 - c

    def pidx(yy, xx, cc):
        return yy * 4 + xx * 2 + cc

    def slot(yy, xx, cc):
        return yy * 4 + cc * 2 + xx

    partner = pidx(y, x, pc)
    my_slot = slot(y, x, c)

    def rcopy(src, dst, ssem, rsem, rr, pp):
        return pltpu.make_async_remote_copy(
            src_ref=src, dst_ref=dst, send_sem=ssem, recv_sem=rsem,
            device_id=(rr, pp), device_id_type=MESH,
        )

    barrier = pltpu.get_barrier_semaphore()
    for j in range(1, R):
        pl.semaphore_signal(barrier, inc=1, device_id=((r + j) % R, p), device_id_type=MESH)
    for j in range(1, NP):
        pl.semaphore_signal(barrier, inc=1, device_id=(r, (p + j) % NP), device_id_type=MESH)
    loads = (
        pltpu.make_async_copy(tea_hbm, tea.at[my_slot], load_sem.at[0]),
        pltpu.make_async_copy(stu_hbm, stu.at[my_slot], load_sem.at[1]),
        pltpu.make_async_copy(pro_hbm, proto, load_sem.at[2]),
    )
    for copy in loads:
        copy.start()
    loads[0].wait()
    loads[1].wait()
    pl.semaphore_wait(barrier, R - 1 + NP - 1)

    sends = []

    def start(copy):
        copy.start()
        sends.append(copy)

    peers = [(dy, dx) for dy in (1, 3, 0, 2) for dx in (0, 1) if (dy, dx) != (0, 0)]
    peers.sort(key=lambda q: ((0, 1, 2, 1)[q[0]] + q[1]))
    bufs = (tea, stu)

    def gather_start(a):
        buf = bufs[a]
        mine = buf.at[my_slot]
        start(rcopy(mine, mine, g_send.at[a, 0], g_recv.at[a, my_slot], r, partner))
        for dy, dx in peers:
            start(rcopy(mine, mine, g_send.at[a, 1 + dy * 2 + dx], g_recv.at[a, my_slot],
                        r, pidx((y + dy) % Y, (x + dx) % 2, c)))

    def gather_wait(a, q):
        block = bufs[a].at[q]
        rcopy(block, block, g_send.at[a, 0], g_recv.at[a, q], r, partner).wait_recv()

    def gather_direct(a, dy):
        ys = (y + dy) % Y
        for dx in (0, 1):
            if (dy, dx) == (0, 0):
                continue
            q = slot(ys, (x + dx) % 2, c)
            gather_wait(a, q)
            block = bufs[a].at[q]
            start(rcopy(block, block, g_send.at[a, 8 + dy * 2 + dx], g_recv.at[a, q], r, partner))

    def gather_passed(a, dy):
        ys = (y + dy) % Y
        for dx in (0, 1):
            gather_wait(a, slot(ys, dx, pc))

    gather_start(0)
    gather_start(1)

    loads[2].wait()

    def norm_step(t, carry):
        cols = pl.ds(pl.multiple_of(t * 256, 256), 256)
        v = proto[:, cols].astype(jnp.float32)
        total = jnp.sum(v * v, axis=0, keepdims=True)
        rnorm[:, cols] = jnp.broadcast_to(1.0 / jnp.sqrt(total + EPSILON), (8, 256))
        return carry

    lax.fori_loop(0, K // 256, norm_step, 0)

    def column_send(it, ch):
        piece = pl.ds(ch * CT, CT)
        mine = colr.at[it, r, piece]
        for j in range(1, R):
            start(rcopy(mine, mine, c_send.at[it, ch, j], c_recv.at[it, ch, r], (r + j) % R, p))

    def column_wait(it, ch):
        piece = pl.ds(ch * CT, CT)
        for j in range(1, R):
            rr = (r + j) % R
            theirs = colr.at[it, rr, piece]
            rcopy(theirs, theirs, c_send.at[it, ch, j], c_recv.at[it, ch, rr], rr, p).wait_recv()
        total = colr[it, 0, piece]
        for j in range(1, R):
            total = total + colr[it, j, piece]
        inverse = 1.0 / total
        for t in range(CT):
            invb[:, pl.ds(ch * CW + t * LANES, LANES)] = jnp.broadcast_to(
                inverse[t : t + 1, :], (8, LANES)
            )

    order = (0, 1, 3, 2)
    for s in range(4):
        if s == 0:
            gather_direct(0, order[0])
        if s < 3:
            gather_direct(0, order[s + 1])
        gather_passed(0, order[s])
        ys = (y + order[s]) % Y
        row0 = pl.multiple_of(ys * PLANE, PLANE)
        rows = pl.ds(row0, PLANE)
        plane = tea[pl.ds(ys * 4, 4)].reshape(PLANE, D)
        wide = plane.astype(jnp.float32)
        total = jnp.sum(wide * wide, axis=1, keepdims=True)
        scale = (LOG2E / TEACHER_TEMP) / jnp.sqrt(total + EPSILON)
        tscale[rows, :] = jnp.broadcast_to(scale, (PLANE, LANES))

        def exp_step(t, carry, s=s, ys=ys, rows=rows):
            cols = pl.ds(pl.multiple_of(t * KE, KE), KE)
            block = tea[pl.ds(ys * 4, 4)].reshape(PLANE, D)
            dots = jnp.dot(block, proto[:, cols], preferred_element_type=jnp.float32)
            rn = rnorm[:, cols]
            row_scale = tscale[rows, :].reshape(PLANE // 8, 8, LANES)
            for j in range(KE // LANES):
                part = dots[:, j * LANES : (j + 1) * LANES].reshape(PLANE // 8, 8, LANES)
                value = jnp.exp2(part * row_scale * rn[None, :, j * LANES : (j + 1) * LANES])
                where = pl.ds(pl.multiple_of(t * KE + j * LANES, LANES), LANES)
                exps[rows, where] = value.reshape(PLANE, LANES)
                added = jnp.sum(value, axis=0)
                if s == 0:
                    colp[:, where] = added
                else:
                    colp[:, where] = colp[:, where] + added
            return carry

        if s < 3:
            lax.fori_loop(0, K // KE, exp_step, 0)
        else:
            for ch in range(NCH):
                lax.fori_loop(ch * CW // KE, (ch + 1) * CW // KE, exp_step, 0)
                for t in range(CT):
                    k = ch * CT + t
                    colr[0, r, k : k + 1, :] = jnp.sum(
                        colp[:, k * LANES : (k + 1) * LANES], axis=0, keepdims=True
                    )
                column_send(0, ch)

    for dy in order:
        gather_direct(1, dy)

    def half_step(t, carry):
        cols = pl.ds(pl.multiple_of(t * 256, 256), 256)
        rn = jnp.broadcast_to(rnorm[0:1, cols], (D, 256))
        half[:, cols] = (proto[:, cols].astype(jnp.float32) * rn).astype(jnp.bfloat16)
        return carry

    lax.fori_loop(0, K // 256, half_step, 0)
    for dy in order:
        gather_passed(1, dy)

    def unit_step(t, carry):
        wide = stu[t].astype(jnp.float32)
        total = jnp.sum(wide * wide, axis=1, keepdims=True)
        unit[pl.ds(pl.multiple_of(t * OWN, OWN), OWN), :] = (
            wide / jnp.sqrt(total + EPSILON)
        ).astype(jnp.bfloat16)
        return carry

    lax.fori_loop(0, NP, unit_step, 0)

    def student_piece(k):
        cols = pl.ds(k * KE, KE)

        def step(b, carry):
            rows = pl.ds(pl.multiple_of(b * PLANE, PLANE), PLANE)
            logits = jnp.dot(unit[rows, :], half[:, cols], preferred_element_type=jnp.float32)
            value = jnp.exp2(logits * (LOG2E / STUDENT_TEMP))
            total = value[:, :LANES]
            for j in range(1, KE // LANES):
                total = total + value[:, j * LANES : (j + 1) * LANES]
            product = lax.dot_general(
                value.astype(jnp.bfloat16), half[:, cols], NT, preferred_element_type=jnp.float32
            )
            if k == 0:
                sacc[rows, :] = total
                ga[rows, :] = product
            else:
                sacc[rows, :] = sacc[rows, :] + total
                ga[rows, :] = ga[rows, :] + product
            return carry

        lax.fori_loop(0, ROWS // PLANE, step, 0)

    def row_pass(ch):
        def step(g, carry):
            rows = pl.ds(pl.multiple_of(g * 64, 64), 64)
            acc = jnp.zeros((8, 8, LANES), jnp.float32)
            if ch > 0:
                acc = racc[rows, :].reshape(8, 8, LANES)
            for j in range(CT):
                where = pl.ds(ch * CW + j * LANES, LANES)
                acc = acc + exps[rows, where].reshape(8, 8, LANES) * invb[:, where][None]
            racc[rows, :] = acc.reshape(64, LANES)
            return carry

        lax.fori_loop(0, ROWS // 64, step, 0)

    def row_send(it):
        for t in range(8):
            rowr[it, my_slot, t : t + 1, :] = jnp.sum(
                racc[t * LANES : (t + 1) * LANES, :].T, axis=0, keepdims=True
            )
        mine = rowr.at[it, my_slot]
        for j in range(1, NP):
            start(rcopy(mine, mine, r_send.at[it, j], r_recv.at[it, my_slot], r, (p + j) % NP))

    def row_wait(it):
        for j in range(1, NP):
            q = (p + j) % NP
            theirs = rowr.at[it, slot(q // 4, (q // 2) % 2, q % 2)]
            rcopy(theirs, theirs, r_send.at[it, j],
                  r_recv.at[it, slot(q // 4, (q // 2) % 2, q % 2)], r, q).wait_recv()
        total = rowr[it, 0]
        for j in range(1, NP):
            total = total + rowr[it, j]
        weights = 1.0 / total
        for t in range(8):
            wexp[t * LANES : (t + 1) * LANES, :] = jnp.broadcast_to(
                weights[t : t + 1, :], (LANES, LANES)
            ).T

    def column_pass(it, ch):
        for h in range(CW // 1024):
            def step(g, accs, h=h):
                rows = pl.ds(pl.multiple_of(g * 64, 64), 64)
                w = wexp[rows, :].reshape(8, 8, LANES)
                out = []
                for j in range(8):
                    where = pl.ds(ch * CW + h * 1024 + j * LANES, LANES)
                    part = exps[rows, where].reshape(8, 8, LANES) * w
                    out.append(accs[j] + jnp.sum(part, axis=0))
                return tuple(out)

            accs = lax.fori_loop(
                0, ROWS // 64, step, tuple(jnp.zeros((8, LANES), jnp.float32) for _ in range(8))
            )
            for j in range(8):
                k = ch * CT + h * 8 + j
                colr[it, r, k : k + 1, :] = jnp.sum(accs[j], axis=0, keepdims=True)
        column_send(it, ch)

    def owner_send(kind, acc, buf, dy):
        ys = (y + dy) % Y
        for t in range(2):
            block = acc[pl.ds(pl.multiple_of(ys * PLANE + t * LANES, LANES), LANES), :]
            buf[ys, my_slot, t : t + 1, :] = jnp.sum(block.T, axis=0, keepdims=True)
        mine = buf.at[ys, my_slot]
        for dx in (0, 1):
            for dc in (0, 1):
                if (dy, dx, dc) == (0, 0, 0):
                    continue
                q = pidx(ys, (x + dx) % 2, (c + dc) % 2)
                start(rcopy(mine, mine, t_send.at[kind, dy * 4 + dx * 2 + dc],
                            t_recv.at[kind, my_slot], r, q))

    def owner_total(kind, buf):
        for j in range(1, NP):
            q = (p + j) % NP
            their = slot(q // 4, (q // 2) % 2, q % 2)
            block = buf.at[y, their]
            rcopy(block, block, t_send.at[kind, j], t_recv.at[kind, their], r, q).wait_recv()
        total = buf[y, 0]
        for j in range(1, NP):
            total = total + buf[y, j]
        for t in range(2):
            own_buf[kind, t * LANES : (t + 1) * LANES, :] = jnp.broadcast_to(
                total[t : t + 1, :], (LANES, LANES)
            ).T
        return own_buf[kind, pl.ds(pl.multiple_of(c * LANES + x * OWN, OWN), OWN), :]

    def pair_copy(kind, g, px, dy):
        ys = (y + dy) % Y
        rows = pl.ds(pl.multiple_of(ys * PLANE + pc * LANES, LANES), LANES)
        return rcopy(g.at[rows], px.at[ys], p_send.at[kind, dy], p_recv.at[kind, dy], r, partner)

    def scatter_send(kind, g, px, ps, rs, dy):
        ys = (y + dy) % Y
        block = px.at[ys]
        rcopy(block, block, p_send.at[kind, dy], p_recv.at[kind, dy], r, partner).wait_recv()
        rows = pl.ds(pl.multiple_of(ys * PLANE + c * LANES, LANES), LANES)
        ps[ys] = g[rows, :] + px[ys]
        for dx in (0, 1):
            if (dy, dx) == (0, 0):
                continue
            xs = (x + dx) % 2
            src = ps.at[ys, pl.ds(pl.multiple_of(xs * OWN, OWN), OWN)]
            start(rcopy(src, rs.at[y * 2 + x], s_send.at[kind, dy * 2 + dx],
                        s_recv.at[kind, y * 2 + x], r, pidx(ys, xs, c)))

    def scatter_total(kind, ps, rs):
        total = ps[y, pl.ds(pl.multiple_of(x * OWN, OWN), OWN), :]
        for dy, dx in peers:
            q = ((y + dy) % Y) * 2 + (x + dx) % 2
            block = rs.at[q]
            rcopy(block, block, s_send.at[kind, dy * 2 + dx], s_recv.at[kind, q], r,
                  partner).wait_recv()
            total = total + rs[q]
        return total

    far_first = (2, 1, 3, 0)

    for k in (0, 1):
        student_piece(k)
    for ch in range(NCH):
        column_wait(0, ch)
        row_pass(ch)
    row_send(0)
    for k in (2, 3, 4):
        student_piece(k)
    row_wait(0)
    for ch in range(NCH):
        column_pass(1, ch)
    for k in (5, 6, 7):
        student_piece(k)
    for ch in range(NCH):
        column_wait(1, ch)
        row_pass(ch)
    row_send(1)
    for dy in far_first:
        start(pair_copy(0, ga, pxa, dy))
    row_wait(1)
    for ch in range(NCH):
        column_pass(2, ch)
        scatter_send(0, ga, pxa, psa, rsa, far_first[ch])
    for dy in far_first:
        owner_send(0, sacc, tota, dy)

    for i, dy in enumerate(far_first):
        ys = (y + dy) % Y
        rows = pl.ds(pl.multiple_of(ys * PLANE, PLANE), PLANE)
        for ch in range(NCH):
            if i == 0:
                column_wait(2, ch)

            def step(t, carry, rows=rows):
                cols = pl.ds(pl.multiple_of(t * KE, KE), KE)
                value = exps[rows, cols].reshape(PLANE // 8, 8, KE) * invb[:, cols][None]
                value = value.reshape(PLANE, KE)
                total = value[:, :LANES]
                for j in range(1, KE // LANES):
                    total = total + value[:, j * LANES : (j + 1) * LANES]
                product = lax.dot_general(
                    value.astype(jnp.bfloat16), half[:, cols], NT,
                    preferred_element_type=jnp.float32,
                )
                racc[rows, :] = racc[rows, :] + total
                gb[rows, :] = gb[rows, :] + product
                return carry

            if ch == 0:
                racc[rows, :] = jnp.zeros((PLANE, LANES), jnp.float32)
                gb[rows, :] = jnp.zeros((PLANE, D), jnp.float32)
            lax.fori_loop(ch * CW // KE, (ch + 1) * CW // KE, step, 0)
        start(pair_copy(1, gb, pxb, dy))
        owner_send(1, racc, totb, dy)
        if i > 0:
            scatter_send(1, gb, pxb, psb, rsb, far_first[i - 1])
    scatter_send(1, gb, pxb, psb, rsb, far_first[3])

    sample_total = owner_total(0, tota)
    first = scatter_total(0, psa, rsa)
    row_total = owner_total(1, totb)
    second = scatter_total(1, psb, rsb)
    weight = 1.0 / row_total
    inv_sample = 1.0 / sample_total
    wide_s = jnp.concatenate([inv_sample, inv_sample], axis=1)
    wide_w = jnp.concatenate([weight, weight], axis=1)
    pulled = second * wide_w
    direction = (first * wide_s - pulled) / STUDENT_TEMP
    floats = stu[my_slot].astype(jnp.float32)
    norm = jnp.sqrt(jnp.sum(floats * floats, axis=1, keepdims=True) + EPSILON)
    own = floats / norm
    half_own = own.astype(jnp.bfloat16).astype(jnp.float32)
    cross = jnp.sum(half_own * pulled, axis=1, keepdims=True) / STUDENT_TEMP
    radial = jnp.sum(own * direction, axis=1, keepdims=True)
    grad_ref[...] = (direction - own * radial) / norm
    loss_ref[...] = jnp.log(sample_total) - jnp.broadcast_to(cross, (OWN, LANES))
    for copy in sends:
        copy.wait_send()


def on_device(teacher_rows, student_rows, prototypes):
    f32, bf16 = jnp.float32, jnp.bfloat16
    vmem = lambda shape, dtype=f32: pltpu.VMEM(shape, dtype)
    dma = lambda *shape: pltpu.SemaphoreType.DMA(shape)
    grads, loss = pl.pallas_call(
        kernel,
        out_shape=(
            jax.ShapeDtypeStruct((OWN, D), f32),
            jax.ShapeDtypeStruct((OWN, LANES), f32),
        ),
        in_specs=[pl.BlockSpec(memory_space=pl.ANY)] * 3,
        out_specs=(pl.BlockSpec(memory_space=pltpu.VMEM), pl.BlockSpec(memory_space=pltpu.VMEM)),
        scratch_shapes=[
            vmem((ROWS, K)),
            vmem((D, K), bf16), vmem((D, K), bf16),
            vmem((NP, OWN, D), bf16), vmem((NP, OWN, D), bf16),
            vmem((ROWS, D), bf16),
            vmem((ROWS, LANES)), vmem((ROWS, LANES)),
            vmem((ROWS, LANES)), vmem((ROWS, LANES)),
            vmem((2, PLANE, LANES)),
            vmem((8, K)), vmem((8, K)), vmem((8, K)),
            vmem((ITERS, R, KT, LANES)),
            vmem((2, NP, 8, LANES)),
            vmem((ROWS, D)), vmem((ROWS, D)),
            vmem((Y, LANES, D)), vmem((Y, LANES, D)),
            vmem((Y, LANES, D)), vmem((Y, LANES, D)),
            vmem((8, OWN, D)), vmem((8, OWN, D)),
            vmem((Y, NP, 2, LANES)), vmem((Y, NP, 2, LANES)),
            dma(3),
            dma(2, 16), dma(2, NP),
            dma(ITERS, NCH, R), dma(ITERS, NCH, R),
            dma(2, NP), dma(2, NP),
            dma(2, NP), dma(2, NP),
            dma(2, Y), dma(2, Y),
            dma(2, 8), dma(2, 8),
        ],
        compiler_params=pltpu.CompilerParams(
            collective_id=0, has_side_effects=True, vmem_limit_bytes=67043328
        ),
        name="prototype_head",
    )(teacher_rows, student_rows, prototypes)
    return grads, loss[:, 0]


def solution(mesh):
    in_specs = (P(("rows", "protos"), None), P(("rows", "protos"), None), P(None, "protos"))
    out_specs = (P(("rows", "protos"), None), P(("rows", "protos")))
    return jax.shard_map(
        on_device, mesh=mesh, in_specs=in_specs, out_specs=out_specs, check_vma=False
    )
```

```python
import contextlib
import math

import jax
import jax.numpy as jnp
from jax import lax
from jax.experimental import pallas as pl
from jax.experimental.pallas import tpu as pltpu
from jax.sharding import PartitionSpec as P

ITERS = 3
EPSILON = 1e-06
TEACHER_TEMP = 0.04
STUDENT_TEMP = 0.1
LOG2E = math.log2(math.e)

R = 8
NP = 16
Y = 4
OWN = 64
PLANE = 256
ROWS = 1024
D = 256
K = 8192
LANES = 128
NCH = 4
CW = K // NCH
CT = CW // LANES
RB = 256
KT = K // LANES
MESH = pl.DeviceIdType.MESH
scope = lambda name: contextlib.nullcontext()
NT = (((1,), (1,)), ((), ()))


def kernel(
    tea_hbm, stu_hbm, pro_hbm,
    grad_ref, loss_ref,
    exps, proto, half, tea, stu, unit,
    tscale, wexp, racc, sacc, own_buf,
    rnorm, invb, colp, colr, rowr,
    ga, gb, pxa, pxb, psa, psb, rsa, rsb, tota, totb, ownd, owns,
    load_sem, g_send, g_recv, c_send, c_recv, r_send, r_recv,
    t_send, t_recv, p_send, p_recv, s_send, s_recv,
):
    r = lax.axis_index("rows")
    p = lax.axis_index("protos")
    y, x, c = p // 4, (p // 2) % 2, p % 2
    pc = 1 - c

    def pidx(yy, xx, cc):
        return yy * 4 + xx * 2 + cc

    def slot(yy, xx, cc):
        return yy * 4 + cc * 2 + xx

    partner = pidx(y, x, pc)
    my_slot = slot(y, x, c)

    def rcopy(src, dst, ssem, rsem, rr, pp):
        return pltpu.make_async_remote_copy(
            src_ref=src, dst_ref=dst, send_sem=ssem, recv_sem=rsem,
            device_id=(rr, pp), device_id_type=MESH,
        )

    barrier = pltpu.get_barrier_semaphore()
    for j in range(1, R):
        pl.semaphore_signal(barrier, inc=1, device_id=((r + j) % R, p), device_id_type=MESH)
    for j in range(1, NP):
        pl.semaphore_signal(barrier, inc=1, device_id=(r, (p + j) % NP), device_id_type=MESH)
    loads = (
        pltpu.make_async_copy(tea_hbm, tea.at[my_slot], load_sem.at[0]),
        pltpu.make_async_copy(stu_hbm, stu.at[my_slot], load_sem.at[1]),
        pltpu.make_async_copy(pro_hbm, proto, load_sem.at[2]),
    )
    for copy in loads:
        copy.start()
    loads[0].wait()
    loads[1].wait()
    pl.semaphore_wait(barrier, R - 1 + NP - 1)

    peers = [(0, 1), (1, 0), (3, 0), (1, 1), (3, 1), (2, 0), (2, 1)]
    bufs = (tea, stu)

    def gather_start(a):
        mine = bufs[a].at[my_slot]
        rcopy(mine, mine, g_send.at[a], g_recv.at[a, 1, y], r, partner).start()
        for dy, dx in peers:
            rcopy(mine, mine, g_send.at[a], g_recv.at[a, 0, y],
                  r, pidx((y + dy) % Y, (x + dx) % 2, c)).start()

    def gather_direct(a, dy):
        ys = (y + dy) % Y
        if dy == 0:
            blocks = bufs[a].at[pl.ds(slot(y, 1 - x, c), 1)]
        else:
            blocks = bufs[a].at[pl.ds(slot(ys, 0, c), 2)]
        rcopy(blocks, blocks, g_send.at[a], g_recv.at[a, 0, ys], r, partner).wait_recv()
        for dx in (0, 1):
            if (dy, dx) != (0, 0):
                block = bufs[a].at[slot(ys, (x + dx) % 2, c)]
                rcopy(block, block, g_send.at[a], g_recv.at[a, 1, ys], r, partner).start()

    def gather_passed(a, dy):
        ys = (y + dy) % Y
        blocks = bufs[a].at[pl.ds(slot(ys, 0, pc), 2)]
        rcopy(blocks, blocks, g_send.at[a], g_recv.at[a, 1, ys], r, partner).wait_recv()

    with scope("gather_start"):
        gather_start(0)

    loads[2].wait()

    def norm_step(t, carry):
        cols = pl.ds(pl.multiple_of(t * 512, 512), 512)
        v = proto[:, cols].astype(jnp.float32)
        total = jnp.sum(v * v, axis=0, keepdims=True)
        inverse = 1.0 / jnp.sqrt(total + EPSILON)
        rnorm[:, cols] = jnp.broadcast_to(inverse, (8, 512))
        half[:, cols] = (v * inverse).astype(jnp.bfloat16)
        return carry

    with scope("norms"):
        lax.fori_loop(0, K // 512, norm_step, 0)

    def column_send(it, ch):
        piece = pl.ds(ch * CT, CT)
        mine = colr.at[it, r, piece]
        for j in range(1, R):
            rcopy(mine, mine, c_send, c_recv.at[it, ch], (r + j) % R, p).start()

    def column_wait(it, ch):
        piece = pl.ds(ch * CT, CT)
        theirs = colr.at[it, pl.ds(0, R - 1), piece]
        rcopy(theirs, theirs, c_send, c_recv.at[it, ch], r, p).wait_recv()
        total = colr[it, 0, piece]
        for j in range(1, R):
            total = total + colr[it, j, piece]
        inverse = 1.0 / total
        for t in range(CT):
            invb[ch * CT + t] = jnp.broadcast_to(inverse[t : t + 1, :], (8, LANES))

    order = (0, 1, 3, 2)

    def exp_tiles(rows, block, first, k0, k1):
        dots = jnp.dot(
            block, proto[:, k0 * LANES : k1 * LANES], preferred_element_type=jnp.float32
        )
        row_scale = tscale[rows, :].reshape(PLANE // 8, 8, LANES)
        for k in range(k0, k1):
            part = dots[:, (k - k0) * LANES : (k - k0 + 1) * LANES]
            part = part.reshape(PLANE // 8, 8, LANES)
            value = jnp.exp2(part * row_scale * rnorm[:, k * LANES : (k + 1) * LANES][None])
            exps[k, rows, :] = value.reshape(PLANE, LANES)
            added = jnp.sum(value, axis=0)
            colp[k] = added if first else colp[k] + added

    for s in range(4):
        with scope("gather_wait"):
            if s == 0:
                gather_direct(0, order[0])
            if s < 3:
                gather_direct(0, order[s + 1])
            gather_passed(0, order[s])
        if s == 0:
            gather_start(1)
        with scope("exp_plane"):
            ys = (y + order[s]) % Y
            rows = pl.ds(pl.multiple_of(ys * PLANE, PLANE), PLANE)
            block = tea[pl.ds(ys * 4, 4)].reshape(PLANE, D)
            wide = block.astype(jnp.float32)
            total = jnp.sum(wide * wide, axis=1, keepdims=True)
            scale = (LOG2E / TEACHER_TEMP) / jnp.sqrt(total + EPSILON)
            tscale[rows, :] = jnp.broadcast_to(scale, (PLANE, LANES))
            if s < 3:
                exp_tiles(rows, block, s == 0, 0, KT)
            else:
                for h in range(2):
                    exp_tiles(rows, block, False, h * KT // 2, (h + 1) * KT // 2)
                    for ch in range(h * NCH // 2, (h + 1) * NCH // 2):
                        for k in range(ch * CT, (ch + 1) * CT):
                            colr[0, r, k : k + 1, :] = jnp.sum(colp[k], axis=0, keepdims=True)
                        column_send(0, ch)

    with scope("student_rows"):
        for dy in order:
            gather_direct(1, dy)
        for dy in order:
            gather_passed(1, dy)

        def unit_step(t, carry):
            wide = stu[pl.ds(t * 4, 4)].reshape(PLANE, D).astype(jnp.float32)
            total = jnp.sum(wide * wide, axis=1, keepdims=True)
            unit[pl.ds(pl.multiple_of(t * PLANE, PLANE), PLANE), :] = (
                wide / jnp.sqrt(total + EPSILON)
            ).astype(jnp.bfloat16)
            return carry

        lax.fori_loop(0, Y, unit_step, 0)

    def student_piece(dy):
        ys = (y + dy) % Y
        rows = pl.ds(pl.multiple_of(ys * PLANE, PLANE), PLANE)
        logits = jnp.dot(unit[rows, :], half[...], preferred_element_type=jnp.float32)
        value = jnp.exp2(logits * (LOG2E / STUDENT_TEMP))
        total = value[:, :LANES]
        for k in range(1, KT):
            total = total + value[:, k * LANES : (k + 1) * LANES]
        sacc[rows, :] = total
        ga[rows, :] = lax.dot_general(
            value.astype(jnp.bfloat16), half[...], NT, preferred_element_type=jnp.float32
        )
        pair_copy(0, ga, pxa, dy).start()

    def row_pass(ch):
        def step(g, carry):
            rows = pl.ds(pl.multiple_of(g * RB, RB), RB)
            acc = jnp.zeros((RB // 8, 8, LANES), jnp.float32)
            if ch > 0:
                acc = racc[rows, :].reshape(RB // 8, 8, LANES)
            for k in range(ch * CT, (ch + 1) * CT):
                acc = acc + exps[k, rows, :].reshape(RB // 8, 8, LANES) * invb[k][None]
            racc[rows, :] = acc.reshape(RB, LANES)
            return carry

        lax.fori_loop(0, ROWS // RB, step, 0)

    def row_send(it):
        for t in range(8):
            rowr[it, my_slot, t : t + 1, :] = jnp.sum(
                racc[t * LANES : (t + 1) * LANES, :].T, axis=0, keepdims=True
            )
        mine = rowr.at[it, my_slot]
        for j in range(1, NP):
            rcopy(mine, mine, r_send, r_recv.at[it], r, (p + j) % NP).start()

    def row_wait(it):
        theirs = rowr.at[it, pl.ds(0, NP - 1)]
        rcopy(theirs, theirs, r_send, r_recv.at[it], r, p).wait_recv()
        total = rowr[it, 0]
        for j in range(1, NP):
            total = total + rowr[it, j]
        weights = 1.0 / total
        for t in range(8):
            wexp[t * LANES : (t + 1) * LANES, :] = jnp.broadcast_to(
                weights[t : t + 1, :], (LANES, LANES)
            ).T

    def column_pass(it, ch):
        def step(g, accs):
            rows = pl.ds(pl.multiple_of(g * 128, 128), 128)
            w = wexp[rows, :].reshape(16, 8, LANES)
            return tuple(
                accs[t] + jnp.sum(exps[ch * CT + t, rows, :].reshape(16, 8, LANES) * w, axis=0)
                for t in range(CT)
            )

        accs = lax.fori_loop(
            0, ROWS // 128, step, tuple(jnp.zeros((8, LANES), jnp.float32) for _ in range(CT))
        )
        for t in range(CT):
            k = ch * CT + t
            colr[it, r, k : k + 1, :] = jnp.sum(accs[t], axis=0, keepdims=True)
        column_send(it, ch)

    def owner_send(kind, acc, buf, dy):
        ys = (y + dy) % Y
        for t in range(2):
            block = acc[pl.ds(pl.multiple_of(ys * PLANE + t * LANES, LANES), LANES), :]
            buf[ys, my_slot, t : t + 1, :] = jnp.sum(block.T, axis=0, keepdims=True)
        mine = buf.at[ys, my_slot]
        for dx in (0, 1):
            for dc in (0, 1):
                if (dy, dx, dc) == (0, 0, 0):
                    continue
                q = pidx(ys, (x + dx) % 2, (c + dc) % 2)
                rcopy(mine, mine, t_send.at[kind], t_recv.at[kind], r, q).start()

    def owner_total(kind, buf):
        theirs = buf.at[y, pl.ds(0, NP - 1)]
        rcopy(theirs, theirs, t_send.at[kind], t_recv.at[kind], r, p).wait_recv()
        total = buf[y, 0]
        for j in range(1, NP):
            total = total + buf[y, j]
        for t in range(2):
            own_buf[kind, t * LANES : (t + 1) * LANES, :] = jnp.broadcast_to(
                total[t : t + 1, :], (LANES, LANES)
            ).T
        return own_buf[kind, pl.ds(pl.multiple_of(c * LANES + x * OWN, OWN), OWN), :]

    def pair_copy(kind, g, px, dy):
        ys = (y + dy) % Y
        rows = pl.ds(pl.multiple_of(ys * PLANE + pc * LANES, LANES), LANES)
        return rcopy(g.at[rows], px.at[ys], p_send.at[kind], p_recv.at[kind, dy], r, partner)

    def scatter_send(kind, g, px, ps, rs, dy):
        ys = (y + dy) % Y
        block = px.at[ys]
        rcopy(block, block, p_send.at[kind], p_recv.at[kind, dy], r, partner).wait_recv()
        rows = pl.ds(pl.multiple_of(ys * PLANE + c * LANES, LANES), LANES)
        ps[ys] = g[rows, :] + px[ys]
        for dx in (0, 1):
            if (dy, dx) == (0, 0):
                continue
            xs = (x + dx) % 2
            src = ps.at[ys, pl.ds(pl.multiple_of(xs * OWN, OWN), OWN)]
            rcopy(src, rs.at[y * 2 + x], s_send.at[kind], s_recv.at[kind],
                  r, pidx(ys, xs, c)).start()

    def scatter_total(kind, ps, rs):
        theirs = rs.at[pl.ds(0, 7)]
        rcopy(theirs, theirs, s_send.at[kind], s_recv.at[kind], r, partner).wait_recv()
        total = ps[y, pl.ds(pl.multiple_of(x * OWN, OWN), OWN), :]
        for dy, dx in peers:
            total = total + rs[((y + dy) % Y) * 2 + (x + dx) % 2]
        return total

    far_first = (2, 1, 3, 0)

    with scope("student"):
        student_piece(far_first[0])
    for ch in range(NCH):
        with scope("column_wait"):
            column_wait(0, ch)
        with scope("row_pass"):
            row_pass(ch)
    with scope("row_send"):
        row_send(0)
    with scope("student"):
        student_piece(far_first[1])
        student_piece(far_first[2])
    with scope("row_wait"):
        row_wait(0)
    for ch in range(NCH):
        with scope("column_pass"):
            column_pass(1, ch)
        if ch < 3:
            with scope("scatter_a"):
                scatter_send(0, ga, pxa, psa, rsa, far_first[ch])
    with scope("student"):
        student_piece(far_first[3])
    for ch in range(NCH):
        with scope("column_wait"):
            column_wait(1, ch)
        with scope("row_pass"):
            row_pass(ch)
        if ch == 0:
            with scope("scatter_a"):
                scatter_send(0, ga, pxa, psa, rsa, far_first[3])
    with scope("row_send"):
        row_send(1)
    with scope("owner_a"):
        for dy in far_first:
            owner_send(0, sacc, tota, dy)
    with scope("row_wait"):
        row_wait(1)
    for ch in range(NCH):
        with scope("column_pass"):
            column_pass(2, ch)

    with scope("student_own"):
        sample_total = owner_total(0, tota)
        first = scatter_total(0, psa, rsa)
        inv_sample = 1.0 / sample_total
        ownd[...] = first * jnp.concatenate([inv_sample, inv_sample], axis=1)
        owns[...] = jnp.log(sample_total)

    with scope("column_wait"):
        for ch in range(NCH):
            column_wait(2, ch)
    for i, dy in enumerate(far_first):
        with scope("final_plane"):
            ys = (y + dy) % Y
            rows = pl.ds(pl.multiple_of(ys * PLANE, PLANE), PLANE)
            total = jnp.zeros((PLANE, LANES), jnp.float32)
            parts = []
            for k in range(KT):
                part = exps[k, rows, :].reshape(PLANE // 8, 8, LANES) * invb[k][None]
                part = part.reshape(PLANE, LANES)
                total = total + part
                parts.append(part.astype(jnp.bfloat16))
            racc[rows, :] = total
            gb[rows, :] = lax.dot_general(
                jnp.concatenate(parts, axis=1), half[...], NT,
                preferred_element_type=jnp.float32,
            )
        pair_copy(1, gb, pxb, dy).start()
        with scope("owner_b"):
            owner_send(1, racc, totb, dy)
        if i > 0:
            with scope("scatter_b"):
                scatter_send(1, gb, pxb, psb, rsb, far_first[i - 1])
    with scope("scatter_last"):
        scatter_send(1, gb, pxb, psb, rsb, far_first[3])

    floats = stu[my_slot].astype(jnp.float32)
    norm = jnp.sqrt(jnp.sum(floats * floats, axis=1, keepdims=True) + EPSILON)
    own = floats / norm
    half_own = own.astype(jnp.bfloat16).astype(jnp.float32)
    with scope("row_total"):
        weight = 1.0 / owner_total(1, totb)
    with scope("last_wait"):
        second = scatter_total(1, psb, rsb)
    with scope("finish"):
        pulled = second * jnp.concatenate([weight, weight], axis=1)
        direction = (ownd[...] - pulled) / STUDENT_TEMP
        cross = jnp.sum(half_own * pulled, axis=1, keepdims=True) / STUDENT_TEMP
        radial = jnp.sum(own * direction, axis=1, keepdims=True)
        grad_ref[...] = (direction - own * radial) / norm
        loss_ref[...] = owns[...] - jnp.broadcast_to(cross, (OWN, LANES))

    def sent(ref, sem):
        rcopy(ref, ref, sem, sem, r, partner).wait_send()

    with scope("sent"):
        sent(tea.at[pl.ds(0, 15)], g_send.at[0])
        sent(stu.at[pl.ds(0, 15)], g_send.at[1])
        sent(colr.at[:, pl.ds(0, R - 1)], c_send)
        sent(rowr.at[:, pl.ds(0, NP - 1)], r_send)
        for kind, (tot, px, rs) in enumerate(((tota, pxa, rsa), (totb, pxb, rsb))):
            sent(tot.at[0, pl.ds(0, NP - 1)], t_send.at[kind])
            sent(px, p_send.at[kind])
            sent(rs.at[pl.ds(0, 7)], s_send.at[kind])


def on_device(teacher_rows, student_rows, prototypes):
    f32, bf16 = jnp.float32, jnp.bfloat16
    vmem = lambda shape, dtype=f32: pltpu.VMEM(shape, dtype)
    dma = lambda *shape: pltpu.SemaphoreType.DMA(shape)
    grads, loss = pl.pallas_call(
        kernel,
        out_shape=(
            jax.ShapeDtypeStruct((OWN, D), f32),
            jax.ShapeDtypeStruct((OWN, LANES), f32),
        ),
        in_specs=[pl.BlockSpec(memory_space=pl.ANY)] * 3,
        out_specs=(pl.BlockSpec(memory_space=pltpu.VMEM), pl.BlockSpec(memory_space=pltpu.VMEM)),
        scratch_shapes=[
            vmem((KT, ROWS, LANES)),
            vmem((D, K), bf16), vmem((D, K), bf16),
            vmem((NP, OWN, D), bf16), vmem((NP, OWN, D), bf16),
            vmem((ROWS, D), bf16),
            vmem((ROWS, LANES)), vmem((ROWS, LANES)),
            vmem((ROWS, LANES)), vmem((ROWS, LANES)),
            vmem((2, PLANE, LANES)),
            vmem((8, K)), vmem((KT, 8, LANES)), vmem((KT, 8, LANES)),
            vmem((ITERS, R, KT, LANES)),
            vmem((2, NP, 8, LANES)),
            vmem((ROWS, D)), vmem((ROWS, D)),
            vmem((Y, LANES, D)), vmem((Y, LANES, D)),
            vmem((Y, LANES, D)), vmem((Y, LANES, D)),
            vmem((8, OWN, D)), vmem((8, OWN, D)),
            vmem((Y, NP, 2, LANES)), vmem((Y, NP, 2, LANES)),
            vmem((OWN, D)), vmem((OWN, LANES)),
            dma(3),
            dma(2), dma(2, 2, Y),
            pltpu.SemaphoreType.DMA, dma(ITERS, NCH),
            pltpu.SemaphoreType.DMA, dma(2),
            dma(2), dma(2),
            dma(2), dma(2, Y),
            dma(2), dma(2),
        ],
        compiler_params=pltpu.CompilerParams(
            collective_id=0, has_side_effects=True, vmem_limit_bytes=67043328
        ),
        name="prototype_head",
    )(teacher_rows, student_rows, prototypes)
    return grads, loss[:, 0]


def solution(mesh):
    in_specs = (P(("rows", "protos"), None), P(("rows", "protos"), None), P(None, "protos"))
    out_specs = (P(("rows", "protos"), None), P(("rows", "protos")))
    return jax.shard_map(
        on_device, mesh=mesh, in_specs=in_specs, out_specs=out_specs, check_vma=False
    )
```

```python
import contextlib
import math

import jax
import jax.numpy as jnp
from jax import lax
from jax.experimental import pallas as pl
from jax.experimental.pallas import tpu as pltpu
from jax.sharding import PartitionSpec as P

ITERS = 3
EPSILON = 1e-06
TEACHER_TEMP = 0.04
STUDENT_TEMP = 0.1
LOG2E = math.log2(math.e)

R = 8
NP = 16
Y = 4
OWN = 64
PLANE = 256
ROWS = 1024
D = 256
K = 8192
LANES = 128
NCH = 4
CW = K // NCH
CT = CW // LANES
RB = 256
FB = 64
KT = K // LANES
MESH = pl.DeviceIdType.MESH
scope = lambda name: contextlib.nullcontext()
NT = (((1,), (1,)), ((), ()))


def kernel(
    tea_hbm, stu_hbm, pro_hbm,
    out_ref,
    exps, proto, half, tea, stu, unit,
    tscale, wexp, racc, sacc, own_buf,
    rnorm, invb, colp, colf, colr, rowr,
    ga, gb, pxa, pxb, psa, psb, rsa, rsb, fwa, fwb, tota, totb, ownd, owns,
    load_sem, g_send, g_recv, c_send, c_recv, r_send, r_recv,
    t_send, t_recv, p_send, p_recv, s_send, s_recv, f_recv,
):
    r = lax.axis_index("rows")
    p = lax.axis_index("protos")
    y, x, c = p // 4, (p // 2) % 2, p % 2
    pc = 1 - c

    def pidx(yy, xx, cc):
        return yy * 4 + xx * 2 + cc

    def slot(yy, xx, cc):
        return yy * 4 + cc * 2 + xx

    apart = pl.when(p >= 0)
    partner = pidx(y, x, pc)
    my_slot = slot(y, x, c)

    def rcopy(src, dst, ssem, rsem, rr, pp):
        return pltpu.make_async_remote_copy(
            src_ref=src, dst_ref=dst, send_sem=ssem, recv_sem=rsem,
            device_id=(rr, pp), device_id_type=MESH,
        )

    barrier = pltpu.get_barrier_semaphore()
    for j in range(1, R):
        pl.semaphore_signal(barrier, inc=1, device_id=((r + j) % R, p), device_id_type=MESH)
    for j in range(1, NP):
        pl.semaphore_signal(barrier, inc=1, device_id=(r, (p + j) % NP), device_id_type=MESH)
    loads = (
        pltpu.make_async_copy(tea_hbm, tea.at[my_slot], load_sem.at[0]),
        pltpu.make_async_copy(stu_hbm, stu.at[my_slot], load_sem.at[1]),
        pltpu.make_async_copy(pro_hbm, proto, load_sem.at[2]),
    )
    for copy in loads:
        copy.start()
    loads[0].wait()
    loads[1].wait()
    pl.semaphore_wait(barrier, R - 1 + NP - 1)

    peers = [(0, 1), (1, 0), (3, 0), (1, 1), (3, 1), (2, 0), (2, 1)]
    bufs = (tea, stu)

    def gather_start(a):
        mine = bufs[a].at[my_slot]
        rcopy(mine, mine, g_send.at[a], g_recv.at[a, 1, y], r, partner).start()
        for dy, dx in peers:
            rcopy(mine, mine, g_send.at[a], g_recv.at[a, 0, y],
                  r, pidx((y + dy) % Y, (x + dx) % 2, c)).start()

    def gather_direct(a, dy):
        ys = (y + dy) % Y
        if dy == 0:
            blocks = bufs[a].at[pl.ds(slot(y, 1 - x, c), 1)]
        else:
            blocks = bufs[a].at[pl.ds(slot(ys, 0, c), 2)]
        rcopy(blocks, blocks, g_send.at[a], g_recv.at[a, 0, ys], r, partner).wait_recv()
        for dx in (0, 1):
            if (dy, dx) != (0, 0):
                block = bufs[a].at[slot(ys, (x + dx) % 2, c)]
                rcopy(block, block, g_send.at[a], g_recv.at[a, 1, ys], r, partner).start()

    def gather_passed(a, dy):
        ys = (y + dy) % Y
        blocks = bufs[a].at[pl.ds(slot(ys, 0, pc), 2)]
        rcopy(blocks, blocks, g_send.at[a], g_recv.at[a, 1, ys], r, partner).wait_recv()

    with scope("gather_start"):
        gather_start(0)

    loads[2].wait()

    def norm_step(t, carry):
        cols = pl.ds(pl.multiple_of(t * 512, 512), 512)
        v = proto[:, cols].astype(jnp.float32)
        total = jnp.sum(v * v, axis=0, keepdims=True)
        inverse = 1.0 / jnp.sqrt(total + EPSILON)
        rnorm[:, cols] = jnp.broadcast_to(inverse, (8, 512))
        half[:, cols] = (v * inverse).astype(jnp.bfloat16)
        return carry

    with scope("norms"):
        lax.fori_loop(0, K // 512, norm_step, 0)

    def column_send(it, ch):
        piece = pl.ds(ch * CT, CT)
        colr[it, r, piece] = colf[piece, :].astype(jnp.bfloat16)
        mine = colr.at[it, r, piece]
        for j in range(1, R):
            rcopy(mine, mine, c_send, c_recv.at[it, ch], (r + j) % R, p).start()

    def column_wait(it, ch):
        piece = pl.ds(ch * CT, CT)
        theirs = colr.at[it, pl.ds(0, R - 1), piece]
        rcopy(theirs, theirs, c_send, c_recv.at[it, ch], r, p).wait_recv()
        total = colr[it, 0, piece].astype(jnp.float32)
        for j in range(1, R):
            total = total + colr[it, j, piece].astype(jnp.float32)
        inverse = 1.0 / total
        for t in range(CT):
            invb[ch * CT + t] = jnp.broadcast_to(inverse[t : t + 1, :], (8, LANES))

    order = (0, 1, 3, 2)

    def exp_tiles(rows, block, first, k0, k1):
        dots = jnp.dot(
            block[...].reshape(PLANE, D), proto[:, k0 * LANES : k1 * LANES],
            preferred_element_type=jnp.float32,
        )
        row_scale = tscale[rows, :].reshape(PLANE // 8, 8, LANES)
        for k in range(k0, k1):
            part = dots[:, (k - k0) * LANES : (k - k0 + 1) * LANES]
            part = part.reshape(PLANE // 8, 8, LANES)
            value = jnp.exp2(part * row_scale * rnorm[:, k * LANES : (k + 1) * LANES][None])
            exps[k, rows, :] = value.reshape(PLANE, LANES)
            added = jnp.sum(value, axis=0)
            colp[k] = added if first else colp[k] + added

    for s in range(4):
        with scope("gather_wait"):
            if s == 0:
                gather_direct(0, order[0])
            if s < 3:
                gather_direct(0, order[s + 1])
            gather_passed(0, order[s])
        if s == 0:
            gather_start(1)
        with scope("exp_plane"):
            ys = (y + order[s]) % Y
            rows = pl.ds(pl.multiple_of(ys * PLANE, PLANE), PLANE)
            block = tea.at[pl.ds(ys * 4, 4)]
            wide = block[...].reshape(PLANE, D).astype(jnp.float32)
            total = jnp.sum(wide * wide, axis=1, keepdims=True)
            scale = (LOG2E / TEACHER_TEMP) / jnp.sqrt(total + EPSILON)
            tscale[rows, :] = jnp.broadcast_to(scale, (PLANE, LANES))
            if s < 3:
                apart(lambda: exp_tiles(rows, block, s == 0, 0, KT))
            else:
                for h in range(2):
                    apart(lambda: exp_tiles(rows, block, False, h * KT // 2, (h + 1) * KT // 2))
                    for ch in range(h * NCH // 2, (h + 1) * NCH // 2):
                        for k in range(ch * CT, (ch + 1) * CT):
                            colf[k : k + 1, :] = jnp.sum(colp[k], axis=0, keepdims=True)
                        column_send(0, ch)

    with scope("student_rows"):
        for dy in order:
            gather_direct(1, dy)
        for dy in order:
            gather_passed(1, dy)

        def unit_step(t, carry):
            wide = stu[pl.ds(t * 4, 4)].reshape(PLANE, D).astype(jnp.float32)
            total = jnp.sum(wide * wide, axis=1, keepdims=True)
            unit[pl.ds(pl.multiple_of(t * PLANE, PLANE), PLANE), :] = (
                wide / jnp.sqrt(total + EPSILON)
            ).astype(jnp.bfloat16)
            return carry

        lax.fori_loop(0, Y, unit_step, 0)

    def student_piece(dy):
        ys = (y + dy) % Y
        rows = pl.ds(pl.multiple_of(ys * PLANE, PLANE), PLANE)

        @apart
        def _():
            logits = jnp.dot(unit[rows, :], half[...], preferred_element_type=jnp.float32)
            value = jnp.exp2(logits * (LOG2E / STUDENT_TEMP))
            total = value[:, :LANES]
            for k in range(1, KT):
                total = total + value[:, k * LANES : (k + 1) * LANES]
            sacc[rows, :] = total
            ga[rows, :] = lax.dot_general(
                value.astype(jnp.bfloat16), half[...], NT, preferred_element_type=jnp.float32
            )

        pair_copy(0, ga, pxa, dy).start()

    def row_pass(ch):
        def step(g, carry):
            rows = pl.ds(pl.multiple_of(g * RB, RB), RB)
            acc = jnp.zeros((RB // 8, 8, LANES), jnp.float32)
            if ch > 0:
                acc = racc[rows, :].reshape(RB // 8, 8, LANES)
            for k in range(ch * CT, (ch + 1) * CT):
                acc = acc + exps[k, rows, :].reshape(RB // 8, 8, LANES) * invb[k][None]
            racc[rows, :] = acc.reshape(RB, LANES)
            return carry

        lax.fori_loop(0, ROWS // RB, step, 0)

    def row_send(it):
        for t in range(8):
            rowr[it, my_slot, t : t + 1, :] = jnp.sum(
                racc[t * LANES : (t + 1) * LANES, :].T, axis=0, keepdims=True
            )
        mine = rowr.at[it, my_slot]
        for j in range(1, NP):
            rcopy(mine, mine, r_send, r_recv.at[it], r, (p + j) % NP).start()

    def row_wait(it):
        theirs = rowr.at[it, pl.ds(0, NP - 1)]
        rcopy(theirs, theirs, r_send, r_recv.at[it], r, p).wait_recv()
        total = rowr[it, 0]
        for j in range(1, NP):
            total = total + rowr[it, j]
        weights = 1.0 / total
        for t in range(8):
            wexp[t * LANES : (t + 1) * LANES, :] = jnp.broadcast_to(
                weights[t : t + 1, :], (LANES, LANES)
            ).T

    def column_pass(it, ch):
        def step(g, accs):
            rows = pl.ds(pl.multiple_of(g * 128, 128), 128)
            w = wexp[rows, :].reshape(16, 8, LANES)
            return tuple(
                accs[t] + jnp.sum(exps[ch * CT + t, rows, :].reshape(16, 8, LANES) * w, axis=0)
                for t in range(CT)
            )

        accs = lax.fori_loop(
            0, ROWS // 128, step, tuple(jnp.zeros((8, LANES), jnp.float32) for _ in range(CT))
        )
        for t in range(CT):
            k = ch * CT + t
            colf[k : k + 1, :] = jnp.sum(accs[t], axis=0, keepdims=True)
        column_send(it, ch)

    def owner_send(kind, acc, buf, dy):
        ys = (y + dy) % Y
        for t in range(2):
            block = acc[pl.ds(pl.multiple_of(ys * PLANE + t * LANES, LANES), LANES), :]
            buf[ys, my_slot, t : t + 1, :] = jnp.sum(block.T, axis=0, keepdims=True)
        mine = buf.at[ys, my_slot]
        for dx in (0, 1):
            for dc in (0, 1):
                if (dy, dx, dc) == (0, 0, 0):
                    continue
                q = pidx(ys, (x + dx) % 2, (c + dc) % 2)
                rcopy(mine, mine, t_send.at[kind], t_recv.at[kind], r, q).start()

    def owner_total(kind, buf):
        theirs = buf.at[y, pl.ds(0, NP - 1)]
        rcopy(theirs, theirs, t_send.at[kind], t_recv.at[kind], r, p).wait_recv()
        total = buf[y, 0]
        for j in range(1, NP):
            total = total + buf[y, j]
        for t in range(2):
            own_buf[kind, t * LANES : (t + 1) * LANES, :] = jnp.broadcast_to(
                total[t : t + 1, :], (LANES, LANES)
            ).T
        return own_buf[kind, pl.ds(pl.multiple_of(c * LANES + x * OWN, OWN), OWN), :]

    def pair_copy(kind, g, px, dy):
        ys = (y + dy) % Y
        rows = pl.ds(pl.multiple_of(ys * PLANE + pc * LANES, LANES), LANES)
        return rcopy(g.at[rows], px.at[ys], p_send.at[kind], p_recv.at[kind, dy], r, partner)

    def scatter_send(kind, dy):
        g, px, ps, rs, fw = products[kind]
        ys = (y + dy) % Y
        block = px.at[ys]
        rcopy(block, block, p_send.at[kind], p_recv.at[kind, dy], r, partner).wait_recv()
        rows = pl.ds(pl.multiple_of(ys * PLANE + c * LANES, LANES), LANES)
        ps[ys] = g[rows, :] + px[ys]
        part = [pl.ds(pl.multiple_of((x + dx) % 2 * OWN, OWN), OWN) for dx in (0, 1)]
        if dy == 2:
            for dx, side in ((0, 3), (1, 1)):
                rcopy(ps.at[ys, part[dx]], fw.at[dx], s_send.at[kind], f_recv.at[kind, dx],
                      r, pidx((y + side) % Y, x, c)).start()
            return
        if dy in (1, 3):
            dx = 1 if dy == 1 else 0
            rcopy(fw.at[dx], fw.at[dx], s_send.at[kind], f_recv.at[kind, dx],
                  r, partner).wait_recv()
            ps[ys, part[dx], :] = ps[ys, part[dx], :] + fw[dx]
        for dx in (0, 1):
            if (dy, dx) != (0, 0):
                rcopy(ps.at[ys, part[dx]], rs.at[y * 2 + x], s_send.at[kind], s_recv.at[kind],
                      r, pidx(ys, (x + dx) % 2, c)).start()

    def scatter_total(kind):
        g, px, ps, rs, fw = products[kind]
        theirs = rs.at[pl.ds(0, 5)]
        rcopy(theirs, theirs, s_send.at[kind], s_recv.at[kind], r, partner).wait_recv()
        rows = pl.ds(pl.multiple_of(my_slot * OWN, OWN), OWN)
        total = g[rows, :] + px[y, pl.ds(pl.multiple_of(x * OWN, OWN), OWN), :]
        for dy, dx in peers:
            if dy != 2:
                total = total + rs[((y + dy) % Y) * 2 + (x + dx) % 2]
        return total

    products = ((ga, pxa, psa, rsa, fwa), (gb, pxb, psb, rsb, fwb))
    far_first = (2, 1, 3, 0)

    with scope("student"):
        student_piece(far_first[0])
    for ch in range(NCH):
        with scope("column_wait"):
            column_wait(0, ch)
        if ch == 1:
            with scope("scatter_a"):
                scatter_send(0, far_first[0])
        with scope("row_pass"):
            row_pass(ch)
    with scope("row_send"):
        row_send(0)
    with scope("student"):
        student_piece(far_first[1])
        student_piece(far_first[2])
    with scope("row_wait"):
        row_wait(0)
    with scope("scatter_a"):
        scatter_send(0, far_first[1])
        scatter_send(0, far_first[2])
    for ch in range(NCH):
        with scope("column_pass"):
            column_pass(1, ch)
    with scope("student"):
        student_piece(far_first[3])
    for ch in range(NCH):
        with scope("column_wait"):
            column_wait(1, ch)
        if ch == 1:
            with scope("scatter_a"):
                scatter_send(0, far_first[3])
        with scope("row_pass"):
            row_pass(ch)
    with scope("row_send"):
        row_send(1)
    with scope("owner_a"):
        for dy in far_first:
            owner_send(0, sacc, tota, dy)
    with scope("row_wait"):
        row_wait(1)
    for ch in range(NCH):
        with scope("column_pass"):
            column_pass(2, ch)

    def final_scale(row0, ch0, ch1):
        for g in range(PLANE // FB):
            rows = pl.ds(pl.multiple_of(row0 + g * FB, FB), FB)
            total = jnp.zeros((FB, LANES), jnp.float32) if ch0 == 0 else racc[rows, :]
            for k in range(ch0 * CT, ch1 * CT):
                part = exps[k, rows, :].reshape(FB // 8, 8, LANES) * invb[k][None]
                part = part.reshape(FB, LANES)
                total = total + part
                proto[g * FB : (g + 1) * FB, k * LANES : (k + 1) * LANES] = part.astype(
                    jnp.bfloat16
                )
            racc[rows, :] = total

    with scope("student_own"):
        sample_total = owner_total(0, tota)
        first = scatter_total(0)
        inv_sample = 1.0 / sample_total
        ownd[...] = first * jnp.concatenate([inv_sample, inv_sample], axis=1)
        owns[...] = jnp.log(sample_total)

    last_order = (2, 1, 3, 0)
    for i, dy in enumerate(last_order):
        ys = (y + dy) % Y
        row0 = pl.multiple_of(ys * PLANE, PLANE)
        if i == 0:
            for ch in range(NCH):
                with scope("column_wait"):
                    column_wait(2, ch)
                with scope("final_scale"):
                    final_scale(row0, ch, ch + 1)
        with scope("final_plane"):
            @apart
            def _():
                if i > 0:
                    final_scale(row0, 0, NCH)
                gb[pl.ds(row0, PLANE), :] = lax.dot_general(
                    proto[...], half[...], NT, preferred_element_type=jnp.float32
                )
        pair_copy(1, gb, pxb, dy).start()
        with scope("owner_b"):
            owner_send(1, racc, totb, dy)
        if i == 1:
            with scope("scatter_b"):
                scatter_send(1, last_order[0])
    with scope("scatter_b"):
        scatter_send(1, last_order[1])
        scatter_send(1, last_order[2])
    with scope("scatter_last"):
        scatter_send(1, last_order[3])

    floats = stu[my_slot].astype(jnp.float32)
    norm = jnp.sqrt(jnp.sum(floats * floats, axis=1, keepdims=True) + EPSILON)
    own = floats / norm
    half_own = own.astype(jnp.bfloat16).astype(jnp.float32)
    with scope("row_total"):
        weight = 1.0 / owner_total(1, totb)
    with scope("last_wait"):
        second = scatter_total(1)
    with scope("finish"):
        pulled = second * jnp.concatenate([weight, weight], axis=1)
        direction = (ownd[...] - pulled) / STUDENT_TEMP
        cross = jnp.sum(half_own * pulled, axis=1, keepdims=True) / STUDENT_TEMP
        radial = jnp.sum(own * direction, axis=1, keepdims=True)
        out_ref[:, :D] = (direction - own * radial) / norm
        out_ref[:, D:] = owns[...] - jnp.broadcast_to(cross, (OWN, LANES))

    def sent(ref, sem):
        rcopy(ref, ref, sem, sem, r, partner).wait_send()

    with scope("sent"):
        sent(tea.at[pl.ds(0, 15)], g_send.at[0])
        sent(stu.at[pl.ds(0, 15)], g_send.at[1])
        sent(colr.at[:, pl.ds(0, R - 1)], c_send)
        sent(rowr.at[:, pl.ds(0, NP - 1)], r_send)
        for kind, (tot, px, rs) in enumerate(((tota, pxa, rsa), (totb, pxb, rsb))):
            sent(tot.at[0, pl.ds(0, NP - 1)], t_send.at[kind])
            sent(px, p_send.at[kind])
            sent(rs.at[pl.ds(0, 7)], s_send.at[kind])


def on_device(teacher_rows, student_rows, prototypes):
    f32, bf16 = jnp.float32, jnp.bfloat16
    vmem = lambda shape, dtype=f32: pltpu.VMEM(shape, dtype)
    dma = lambda *shape: pltpu.SemaphoreType.DMA(shape)
    out = pl.pallas_call(
        kernel,
        out_shape=jax.ShapeDtypeStruct((OWN, D + LANES), f32),
        in_specs=[pl.BlockSpec(memory_space=pl.ANY)] * 3,
        out_specs=pl.BlockSpec(memory_space=pltpu.VMEM),
        scratch_shapes=[
            vmem((KT, ROWS, LANES)),
            vmem((D, K), bf16), vmem((D, K), bf16),
            vmem((NP, OWN, D), bf16), vmem((NP, OWN, D), bf16),
            vmem((ROWS, D), bf16),
            vmem((ROWS, LANES)), vmem((ROWS, LANES)),
            vmem((ROWS, LANES)), vmem((ROWS, LANES)),
            vmem((2, PLANE, LANES)),
            vmem((8, K)), vmem((KT, 8, LANES)), vmem((KT, 8, LANES)),
            vmem((KT, LANES)), vmem((ITERS, R, KT, LANES), bf16),
            vmem((2, NP, 8, LANES)),
            vmem((ROWS, D)), vmem((ROWS, D)),
            vmem((Y, LANES, D)), vmem((Y, LANES, D)),
            vmem((Y, LANES, D)), vmem((Y, LANES, D)),
            vmem((8, OWN, D)), vmem((8, OWN, D)),
            vmem((2, OWN, D)), vmem((2, OWN, D)),
            vmem((Y, NP, 2, LANES)), vmem((Y, NP, 2, LANES)),
            vmem((OWN, D)), vmem((OWN, LANES)),
            dma(3),
            dma(2), dma(2, 2, Y),
            pltpu.SemaphoreType.DMA, dma(ITERS, NCH),
            pltpu.SemaphoreType.DMA, dma(2),
            dma(2), dma(2),
            dma(2), dma(2, Y),
            dma(2), dma(2), dma(2, 2),
        ],
        compiler_params=pltpu.CompilerParams(
            collective_id=0, has_side_effects=True, vmem_limit_bytes=67043328
        ),
        name="prototype_head",
    )(teacher_rows, student_rows, prototypes)
    return out[:, :D], out[:, D]


def solution(mesh):
    in_specs = (P(("rows", "protos"), None), P(("rows", "protos"), None), P(None, "protos"))
    out_specs = (P(("rows", "protos"), None), P(("rows", "protos")))
    return jax.shard_map(
        on_device, mesh=mesh, in_specs=in_specs, out_specs=out_specs, check_vma=False
    )
```

```python
import contextlib
import math

import jax
import jax.numpy as jnp
from jax import lax
from jax.experimental import pallas as pl
from jax.experimental.pallas import tpu as pltpu
from jax.sharding import PartitionSpec as P

ITERS = 3
EPSILON = 1e-06
TEACHER_TEMP = 0.04
STUDENT_TEMP = 0.1
LOG2E = math.log2(math.e)

R = 8
NP = 16
Y = 4
OWN = 64
PLANE = 256
ROWS = 1024
D = 256
K = 8192
LANES = 128
NCH = 4
CW = K // NCH
CT = CW // LANES
RB = 256
FB = 64
KT = K // LANES
MESH = pl.DeviceIdType.MESH
scope = lambda name: contextlib.nullcontext()
NT = (((1,), (1,)), ((), ()))


def kernel(
    tea_hbm, stu_hbm, pro_hbm,
    out_ref,
    exps, proto, half, tea, stu, unit,
    tscale, wexp, racc, sacc, own_buf,
    rnorm, invb, colp, colf, colr, rowr,
    ga, gb, pxa, pxb, psa, psb, rsa, rsb, fwa, fwb, tota, totb, ownd, owns,
    load_sem, g_send, g_recv, c_send, c_recv, r_send, r_recv,
    t_send, t_recv, p_send, p_recv, s_send, s_recv, f_recv,
):
    r = lax.axis_index("rows")
    p = lax.axis_index("protos")
    y, x, c = p // 4, (p // 2) % 2, p % 2
    pc = 1 - c

    def pidx(yy, xx, cc):
        return yy * 4 + xx * 2 + cc

    def slot(yy, xx, cc):
        return yy * 4 + cc * 2 + xx

    apart = pl.when(p >= 0)
    partner = pidx(y, x, pc)
    my_slot = slot(y, x, c)

    def rcopy(src, dst, ssem, rsem, rr, pp):
        return pltpu.make_async_remote_copy(
            src_ref=src, dst_ref=dst, send_sem=ssem, recv_sem=rsem,
            device_id=(rr, pp), device_id_type=MESH,
        )

    barrier = pltpu.get_barrier_semaphore()
    for j in range(1, R):
        pl.semaphore_signal(barrier, inc=1, device_id=((r + j) % R, p), device_id_type=MESH)
    for j in range(1, NP):
        pl.semaphore_signal(barrier, inc=1, device_id=(r, (p + j) % NP), device_id_type=MESH)
    loads = (
        pltpu.make_async_copy(tea_hbm, tea.at[my_slot], load_sem.at[0]),
        pltpu.make_async_copy(stu_hbm, stu.at[my_slot], load_sem.at[1]),
        pltpu.make_async_copy(pro_hbm, proto, load_sem.at[2]),
    )
    for copy in loads:
        copy.start()
    loads[0].wait()
    loads[1].wait()
    pl.semaphore_wait(barrier, R - 1 + NP - 1)

    peers = [(0, 1), (1, 0), (3, 0), (1, 1), (3, 1), (2, 0), (2, 1)]
    bufs = (tea, stu)

    def gather_start(a):
        mine = bufs[a].at[my_slot]
        rcopy(mine, mine, g_send.at[a], g_recv.at[a, 1, y], r, partner).start()
        for dy, dx in peers:
            rcopy(mine, mine, g_send.at[a], g_recv.at[a, 0, y],
                  r, pidx((y + dy) % Y, (x + dx) % 2, c)).start()

    def gather_direct(a, dy):
        ys = (y + dy) % Y
        if dy == 0:
            blocks = bufs[a].at[pl.ds(slot(y, 1 - x, c), 1)]
        else:
            blocks = bufs[a].at[pl.ds(slot(ys, 0, c), 2)]
        rcopy(blocks, blocks, g_send.at[a], g_recv.at[a, 0, ys], r, partner).wait_recv()
        for dx in (0, 1):
            if (dy, dx) != (0, 0):
                block = bufs[a].at[slot(ys, (x + dx) % 2, c)]
                rcopy(block, block, g_send.at[a], g_recv.at[a, 1, ys], r, partner).start()

    def gather_passed(a, dy):
        ys = (y + dy) % Y
        blocks = bufs[a].at[pl.ds(slot(ys, 0, pc), 2)]
        rcopy(blocks, blocks, g_send.at[a], g_recv.at[a, 1, ys], r, partner).wait_recv()

    with scope("gather_start"):
        gather_start(0)

    loads[2].wait()

    def norm_step(t, carry):
        cols = pl.ds(pl.multiple_of(t * 512, 512), 512)
        v = proto[:, cols].astype(jnp.float32)
        total = jnp.sum(v * v, axis=0, keepdims=True)
        inverse = 1.0 / jnp.sqrt(total + EPSILON)
        rnorm[:, cols] = jnp.broadcast_to(inverse, (8, 512))
        half[:, cols] = (v * inverse).astype(jnp.bfloat16)
        return carry

    with scope("norms"):
        lax.fori_loop(0, K // 512, norm_step, 0)

    def column_send(it, ch):
        piece = pl.ds(ch * CT, CT)
        colr[it, r, piece] = colf[piece, :].astype(jnp.bfloat16)
        mine = colr.at[it, r, piece]
        for j in range(1, R):
            rcopy(mine, mine, c_send, c_recv.at[it, ch], (r + j) % R, p).start()

    def column_wait(it, ch):
        piece = pl.ds(ch * CT, CT)
        theirs = colr.at[it, pl.ds(0, R - 1), piece]
        rcopy(theirs, theirs, c_send, c_recv.at[it, ch], r, p).wait_recv()
        total = colr[it, 0, piece].astype(jnp.float32)
        for j in range(1, R):
            total = total + colr[it, j, piece].astype(jnp.float32)
        inverse = 1.0 / total
        for t in range(CT):
            invb[ch * CT + t] = jnp.broadcast_to(inverse[t : t + 1, :], (8, LANES))

    order = (0, 1, 3, 2)

    def exp_tiles(rows, block, first, k0, k1):
        dots = jnp.dot(
            block[...].reshape(PLANE, D), proto[:, k0 * LANES : k1 * LANES],
            preferred_element_type=jnp.float32,
        )
        row_scale = tscale[rows, :].reshape(PLANE // 8, 8, LANES)
        for k in range(k0, k1):
            part = dots[:, (k - k0) * LANES : (k - k0 + 1) * LANES]
            part = part.reshape(PLANE // 8, 8, LANES)
            value = jnp.exp2(part * row_scale * rnorm[:, k * LANES : (k + 1) * LANES][None])
            exps[k, rows, :] = value.reshape(PLANE, LANES)
            added = jnp.sum(value, axis=0)
            colp[k] = added if first else colp[k] + added

    for s in range(4):
        with scope("gather_wait"):
            if s == 0:
                gather_direct(0, order[0])
            if s < 3:
                gather_direct(0, order[s + 1])
            gather_passed(0, order[s])
        if s == 0:
            gather_start(1)
        with scope("exp_plane"):
            ys = (y + order[s]) % Y
            rows = pl.ds(pl.multiple_of(ys * PLANE, PLANE), PLANE)
            block = tea.at[pl.ds(ys * 4, 4)]
            wide = block[...].reshape(PLANE, D).astype(jnp.float32)
            total = jnp.sum(wide * wide, axis=1, keepdims=True)
            scale = (LOG2E / TEACHER_TEMP) / jnp.sqrt(total + EPSILON)
            tscale[rows, :] = jnp.broadcast_to(scale, (PLANE, LANES))
            if s < 3:
                apart(lambda: exp_tiles(rows, block, s == 0, 0, KT))
            else:
                for h in range(2):
                    apart(lambda: exp_tiles(rows, block, False, h * KT // 2, (h + 1) * KT // 2))
                    for ch in range(h * NCH // 2, (h + 1) * NCH // 2):
                        for k in range(ch * CT, (ch + 1) * CT):
                            colf[k : k + 1, :] = jnp.sum(colp[k], axis=0, keepdims=True)
                        column_send(0, ch)

    with scope("student_rows"):
        for dy in order:
            gather_direct(1, dy)
        for dy in order:
            gather_passed(1, dy)

        def unit_step(t, carry):
            wide = stu[pl.ds(t * 4, 4)].reshape(PLANE, D).astype(jnp.float32)
            total = jnp.sum(wide * wide, axis=1, keepdims=True)
            unit[pl.ds(pl.multiple_of(t * PLANE, PLANE), PLANE), :] = (
                wide / jnp.sqrt(total + EPSILON)
            ).astype(jnp.bfloat16)
            return carry

        lax.fori_loop(0, Y, unit_step, 0)

    def student_piece(dy):
        ys = (y + dy) % Y
        rows = pl.ds(pl.multiple_of(ys * PLANE, PLANE), PLANE)

        @apart
        def _():
            logits = jnp.dot(unit[rows, :], half[...], preferred_element_type=jnp.float32)
            value = jnp.exp2(logits * (LOG2E / STUDENT_TEMP))
            total = value[:, :LANES]
            for k in range(1, KT):
                total = total + value[:, k * LANES : (k + 1) * LANES]
            sacc[rows, :] = total
            ga[rows, :] = lax.dot_general(
                value.astype(jnp.bfloat16), half[...], NT, preferred_element_type=jnp.float32
            )

        pair_copy(0, ga, pxa, dy).start()

    def row_pass(ch):
        def step(g, carry):
            rows = pl.ds(pl.multiple_of(g * RB, RB), RB)
            acc = jnp.zeros((RB // 8, 8, LANES), jnp.float32)
            if ch > 0:
                acc = racc[rows, :].reshape(RB // 8, 8, LANES)
            for k in range(ch * CT, (ch + 1) * CT):
                acc = acc + exps[k, rows, :].reshape(RB // 8, 8, LANES) * invb[k][None]
            racc[rows, :] = acc.reshape(RB, LANES)
            return carry

        lax.fori_loop(0, ROWS // RB, step, 0)

    def row_send(it):
        for t in range(8):
            rowr[it, my_slot, t : t + 1, :] = jnp.sum(
                racc[t * LANES : (t + 1) * LANES, :].T, axis=0, keepdims=True
            )
        mine = rowr.at[it, my_slot]
        for j in range(1, NP):
            rcopy(mine, mine, r_send, r_recv.at[it], r, (p + j) % NP).start()

    def row_wait(it):
        theirs = rowr.at[it, pl.ds(0, NP - 1)]
        rcopy(theirs, theirs, r_send, r_recv.at[it], r, p).wait_recv()
        total = rowr[it, 0]
        for j in range(1, NP):
            total = total + rowr[it, j]
        weights = 1.0 / total
        for t in range(8):
            wexp[t * LANES : (t + 1) * LANES, :] = jnp.broadcast_to(
                weights[t : t + 1, :], (LANES, LANES)
            ).T

    def column_pass(it, ch):
        def step(g, accs):
            rows = pl.ds(pl.multiple_of(g * 128, 128), 128)
            w = wexp[rows, :].reshape(16, 8, LANES)
            return tuple(
                accs[t] + jnp.sum(exps[ch * CT + t, rows, :].reshape(16, 8, LANES) * w, axis=0)
                for t in range(CT)
            )

        accs = lax.fori_loop(
            0, ROWS // 128, step, tuple(jnp.zeros((8, LANES), jnp.float32) for _ in range(CT))
        )
        for t in range(CT):
            k = ch * CT + t
            colf[k : k + 1, :] = jnp.sum(accs[t], axis=0, keepdims=True)
        column_send(it, ch)

    def owner_send(kind, acc, buf, dy):
        ys = (y + dy) % Y
        for t in range(2):
            block = acc[pl.ds(pl.multiple_of(ys * PLANE + t * LANES, LANES), LANES), :]
            buf[ys, my_slot, t : t + 1, :] = jnp.sum(block.T, axis=0, keepdims=True)
        mine = buf.at[ys, my_slot]
        for dx in (0, 1):
            for dc in (0, 1):
                if (dy, dx, dc) == (0, 0, 0):
                    continue
                q = pidx(ys, (x + dx) % 2, (c + dc) % 2)
                rcopy(mine, mine, t_send.at[kind], t_recv.at[kind], r, q).start()

    def owner_total(kind, buf):
        theirs = buf.at[y, pl.ds(0, NP - 1)]
        rcopy(theirs, theirs, t_send.at[kind], t_recv.at[kind], r, p).wait_recv()
        total = buf[y, 0]
        for j in range(1, NP):
            total = total + buf[y, j]
        for t in range(2):
            own_buf[kind, t * LANES : (t + 1) * LANES, :] = jnp.broadcast_to(
                total[t : t + 1, :], (LANES, LANES)
            ).T
        return own_buf[kind, pl.ds(pl.multiple_of(c * LANES + x * OWN, OWN), OWN), :]

    def pair_copy(kind, g, px, dy):
        ys = (y + dy) % Y
        rows = pl.ds(pl.multiple_of(ys * PLANE + pc * LANES, LANES), LANES)
        return rcopy(g.at[rows], px.at[ys], p_send.at[kind], p_recv.at[kind, dy], r, partner)

    def scatter_send(kind, dy):
        g, px, ps, rs, fw = products[kind]
        ys = (y + dy) % Y
        block = px.at[ys]
        rcopy(block, block, p_send.at[kind], p_recv.at[kind, dy], r, partner).wait_recv()
        rows = pl.ds(pl.multiple_of(ys * PLANE + c * LANES, LANES), LANES)
        ps[ys] = g[rows, :] + px[ys]
        part = [pl.ds(pl.multiple_of((x + dx) % 2 * OWN, OWN), OWN) for dx in (0, 1)]
        if dy == 2:
            for dx, side in ((0, 3), (1, 1)):
                rcopy(ps.at[ys, part[dx]], fw.at[dx], s_send.at[kind], f_recv.at[kind, dx],
                      r, pidx((y + side) % Y, x, c)).start()
            return
        if dy in (1, 3):
            dx = 1 if dy == 1 else 0
            rcopy(fw.at[dx], fw.at[dx], s_send.at[kind], f_recv.at[kind, dx],
                  r, partner).wait_recv()
            ps[ys, part[dx], :] = ps[ys, part[dx], :] + fw[dx]
        for dx in (0, 1):
            if (dy, dx) != (0, 0):
                rcopy(ps.at[ys, part[dx]], rs.at[y * 2 + x], s_send.at[kind], s_recv.at[kind],
                      r, pidx(ys, (x + dx) % 2, c)).start()

    def scatter_total(kind):
        g, px, ps, rs, fw = products[kind]
        theirs = rs.at[pl.ds(0, 5)]
        rcopy(theirs, theirs, s_send.at[kind], s_recv.at[kind], r, partner).wait_recv()
        rows = pl.ds(pl.multiple_of(my_slot * OWN, OWN), OWN)
        total = g[rows, :] + px[y, pl.ds(pl.multiple_of(x * OWN, OWN), OWN), :]
        for dy, dx in peers:
            if dy != 2:
                total = total + rs[((y + dy) % Y) * 2 + (x + dx) % 2]
        return total

    products = ((ga, pxa, psa, rsa, fwa), (gb, pxb, psb, rsb, fwb))
    far_first = (2, 1, 3, 0)

    with scope("student"):
        student_piece(far_first[0])
    for ch in range(NCH):
        with scope("column_wait"):
            column_wait(0, ch)
        if ch == NCH - 1:
            with scope("scatter_a"):
                scatter_send(0, far_first[0])
        with scope("row_pass"):
            row_pass(ch)
    with scope("row_send"):
        row_send(0)
    with scope("student"):
        student_piece(far_first[1])
        student_piece(far_first[2])
    with scope("row_wait"):
        row_wait(0)
    for ch in range(NCH):
        with scope("column_pass"):
            column_pass(1, ch)
        if ch in (0, 1):
            with scope("scatter_a"):
                scatter_send(0, far_first[1 + ch])
    with scope("student"):
        student_piece(far_first[3])
    for ch in range(NCH):
        with scope("column_wait"):
            column_wait(1, ch)
        if ch == 1:
            with scope("scatter_a"):
                scatter_send(0, far_first[3])
        with scope("row_pass"):
            row_pass(ch)
    with scope("row_send"):
        row_send(1)
    with scope("owner_a"):
        for dy in far_first:
            owner_send(0, sacc, tota, dy)
    with scope("row_wait"):
        row_wait(1)
    for ch in range(NCH):
        with scope("column_pass"):
            column_pass(2, ch)

    def final_scale(row0, ch0, ch1):
        for g in range(PLANE // FB):
            rows = pl.ds(pl.multiple_of(row0 + g * FB, FB), FB)
            total = jnp.zeros((FB, LANES), jnp.float32) if ch0 == 0 else racc[rows, :]
            for k in range(ch0 * CT, ch1 * CT):
                part = exps[k, rows, :].reshape(FB // 8, 8, LANES) * invb[k][None]
                part = part.reshape(FB, LANES)
                total = total + part
                proto[g * FB : (g + 1) * FB, k * LANES : (k + 1) * LANES] = part.astype(
                    jnp.bfloat16
                )
            racc[rows, :] = total

    with scope("student_own"):
        sample_total = owner_total(0, tota)
        first = scatter_total(0)
        inv_sample = 1.0 / sample_total
        ownd[...] = first * jnp.concatenate([inv_sample, inv_sample], axis=1)
        owns[...] = jnp.log(sample_total)

    last_order = (2, 1, 3, 0)
    for i, dy in enumerate(last_order):
        ys = (y + dy) % Y
        row0 = pl.multiple_of(ys * PLANE, PLANE)
        if i == 0:
            for ch in range(NCH):
                with scope("column_wait"):
                    column_wait(2, ch)
                with scope("final_scale"):
                    final_scale(row0, ch, ch + 1)
        with scope("final_plane"):
            @apart
            def _():
                if i > 0:
                    final_scale(row0, 0, NCH)
                gb[pl.ds(row0, PLANE), :] = lax.dot_general(
                    proto[...], half[...], NT, preferred_element_type=jnp.float32
                )
        pair_copy(1, gb, pxb, dy).start()
        with scope("owner_b"):
            owner_send(1, racc, totb, dy)
        if i == 1:
            with scope("scatter_b"):
                scatter_send(1, last_order[0])
    with scope("scatter_b"):
        scatter_send(1, last_order[1])
        scatter_send(1, last_order[2])
    with scope("scatter_last"):
        scatter_send(1, last_order[3])

    floats = stu[my_slot].astype(jnp.float32)
    norm = jnp.sqrt(jnp.sum(floats * floats, axis=1, keepdims=True) + EPSILON)
    own = floats / norm
    half_own = own.astype(jnp.bfloat16).astype(jnp.float32)
    with scope("row_total"):
        weight = 1.0 / owner_total(1, totb)
    with scope("last_wait"):
        second = scatter_total(1)
    with scope("finish"):
        pulled = second * jnp.concatenate([weight, weight], axis=1)
        direction = (ownd[...] - pulled) / STUDENT_TEMP
        cross = jnp.sum(half_own * pulled, axis=1, keepdims=True) / STUDENT_TEMP
        radial = jnp.sum(own * direction, axis=1, keepdims=True)
        out_ref[:, :D] = (direction - own * radial) / norm
        out_ref[:, D:] = owns[...] - jnp.broadcast_to(cross, (OWN, LANES))

    def sent(ref, sem):
        rcopy(ref, ref, sem, sem, r, partner).wait_send()

    with scope("sent"):
        sent(tea.at[pl.ds(0, 15)], g_send.at[0])
        sent(stu.at[pl.ds(0, 15)], g_send.at[1])
        sent(colr.at[:, pl.ds(0, R - 1)], c_send)
        sent(rowr.at[:, pl.ds(0, NP - 1)], r_send)
        for kind, (tot, px, rs) in enumerate(((tota, pxa, rsa), (totb, pxb, rsb))):
            sent(tot.at[0, pl.ds(0, NP - 1)], t_send.at[kind])
            sent(px, p_send.at[kind])
            sent(rs.at[pl.ds(0, 7)], s_send.at[kind])


def on_device(teacher_rows, student_rows, prototypes):
    f32, bf16 = jnp.float32, jnp.bfloat16
    vmem = lambda shape, dtype=f32: pltpu.VMEM(shape, dtype)
    dma = lambda *shape: pltpu.SemaphoreType.DMA(shape)
    out = pl.pallas_call(
        kernel,
        out_shape=jax.ShapeDtypeStruct((OWN, D + LANES), f32),
        in_specs=[pl.BlockSpec(memory_space=pl.ANY)] * 3,
        out_specs=pl.BlockSpec(memory_space=pltpu.VMEM),
        scratch_shapes=[
            vmem((KT, ROWS, LANES)),
            vmem((D, K), bf16), vmem((D, K), bf16),
            vmem((NP, OWN, D), bf16), vmem((NP, OWN, D), bf16),
            vmem((ROWS, D), bf16),
            vmem((ROWS, LANES)), vmem((ROWS, LANES)),
            vmem((ROWS, LANES)), vmem((ROWS, LANES)),
            vmem((2, PLANE, LANES)),
            vmem((8, K)), vmem((KT, 8, LANES)), vmem((KT, 8, LANES)),
            vmem((KT, LANES)), vmem((ITERS, R, KT, LANES), bf16),
            vmem((2, NP, 8, LANES)),
            vmem((ROWS, D)), vmem((ROWS, D)),
            vmem((Y, LANES, D)), vmem((Y, LANES, D)),
            vmem((Y, LANES, D)), vmem((Y, LANES, D)),
            vmem((8, OWN, D)), vmem((8, OWN, D)),
            vmem((2, OWN, D)), vmem((2, OWN, D)),
            vmem((Y, NP, 2, LANES)), vmem((Y, NP, 2, LANES)),
            vmem((OWN, D)), vmem((OWN, LANES)),
            dma(3),
            dma(2), dma(2, 2, Y),
            pltpu.SemaphoreType.DMA, dma(ITERS, NCH),
            pltpu.SemaphoreType.DMA, dma(2),
            dma(2), dma(2),
            dma(2), dma(2, Y),
            dma(2), dma(2), dma(2, 2),
        ],
        compiler_params=pltpu.CompilerParams(
            collective_id=0, has_side_effects=True, vmem_limit_bytes=67043328
        ),
        name="prototype_head",
    )(teacher_rows, student_rows, prototypes)
    return out[:, :D], out[:, D]


def solution(mesh):
    in_specs = (P(("rows", "protos"), None), P(("rows", "protos"), None), P(None, "protos"))
    out_specs = (P(("rows", "protos"), None), P(("rows", "protos")))
    return jax.shard_map(
        on_device, mesh=mesh, in_specs=in_specs, out_specs=out_specs, check_vma=False
    )
```
